32 devices in a mesh: groups: 2 (over y), row: 16 (over z, x, core).
Axes of the slice: x: 2, y: 2, z: 4, core: 2. Of those that a mesh axis runs over, the one named last changes fastest.
Arguments:
- object_tiles: bfloat16 [8192, 2, 2048], P(('groups', 'row')), parts along dimension 0, may hold values from -4 to 4
- probe: float32 [4, 256, 2, 256], replicated, may hold values from -3 to 3
- measured: bfloat16 [192, 256, 256], P(('groups', 'row')), parts along dimension 0, may hold values from 0.19921875 to 2.5
- offset_row: int32 [192], P(('groups', 'row')), parts along dimension 0, may hold values from 0 to 255
- offset_col: int32 [192], P(('groups', 'row')), parts along dimension 0, may hold values from 0 to 1791
- subpixel: int32 [192], P(('groups', 'row')), parts along dimension 0, may hold values from 0 to 15
- live_count: int32 [32], P(('groups', 'row')), parts along dimension 0, may hold values from 1 to 6, 48 in all
Outputs:
- object_grad: float32 [8192, 2, 2048], P(('groups', 'row')), parts along dimension 0
- probe_grad: float32 [8, 256, 2, 256], P('groups'), parts along dimension 0
- position_grad: float32 [2, 192], P(None, ('groups', 'row')), parts along dimension 1
The draws below stay inside these ranges and needn't reach their ends.
There are 2 independent parts, one for each index of `groups`. The reference program is written for one: setup_inputs(seed, part) draws one part's arguments, and reference() takes and returns one part's arrays. A program takes and returns all parts, laid end to end along the dimension named above; an argument that names none is the same for every part. Nothing has to cross between parts.
Inputs may be any that keep to these rules, and one draw needn't show every extreme that they name: Device d's live slots are its first live_count[d] slots; live_count sums to 48 and reaches 6 on some device.
All inputs are finite; a program needn't handle non-finite values.
Results may differ from the reference program's by a relative error of at most 0.0099.
Values may be sent and summed in bfloat16 or wider, within the bound.
A program may use at most 128 MiB of HBM per device.

```python
import math
import jax
import jax.numpy as jnp
import numpy as np
from jax import lax

PATCH = 256
MODES = 4
ROWS_DEV = 256
OW = 2048
SLOTS = 6
OH = 4096
NPOS = 96
MINI = 48
N_ROW = 16


def set_ends(array, key, low, high):
    dims = array.shape
    spot = [jax.random.randint(jax.random.fold_in(key, axis), (), 0, dims[axis]) for axis in range(len(dims))]
    array = array.at[tuple(spot)].set(low)
    longest = dims.index(max(dims))
    spot[longest] = (spot[longest] + 1) % dims[longest]
    return array.at[tuple(spot)].set(high)


def block_scale(rng, dims, shards, least, high):
    factor_of = 1.0
    for dim, shards_of in shards:
        heights = jax.random.uniform(jax.random.fold_in(jax.random.fold_in(rng, 6), dim), (shards_of,), jnp.float32, least / len(shards), high / len(shards))
        factor_of = factor_of * jnp.repeat(jnp.exp(heights), dims[dim] // shards_of).reshape((-1,) + (1,) * (len(dims) - 1 - dim))
    return factor_of


def split_up(number_of, total, reach, lean):
    portions = [(1 << 20) // math.isqrt(grade ** lean) + 1 for grade in range(2, number_of + 1)]
    spare, counts = total - reach - (number_of - 1), [1] * (number_of - 1)
    while spare > 0:
        movable = [i for i in range(number_of - 1) if counts[i] < reach]
        mass, budget = sum([portions[i] for i in movable]), spare
        for i in movable:
            more = min(reach - counts[i], max(1, budget * portions[i] // mass), spare)
            counts[i] = counts[i] + more
            spare = spare - more
    return np.array([reach] + counts)


def uneven(stream_key, amount, total, most, lean):
    if amount == 2:
        one = jax.random.randint(stream_key, (), max(1, total - most), min(most, total - 1) + 1)
        return jnp.stack([one, total - one])
    tallies = jnp.asarray(split_up(amount, total, most, lean), jnp.int32)
    pairs = (amount - 1) // 2
    source_of, sink = tallies[1:1 + 2 * pairs:2], tallies[2:2 + 2 * pairs:2]
    slack = jnp.minimum(source_of - 1, most - sink)
    moved = jax.random.randint(jax.random.fold_in(stream_key, 1), (pairs,), 0, 1 << 20) % (slack + 1)
    tallies = tallies.at[1:1 + 2 * pairs:2].set(source_of - moved).at[2:2 + 2 * pairs:2].set(sink + moved)
    return tallies[jax.random.permutation(jax.random.fold_in(stream_key, 2), amount)]


def centred(stream_key, extent, width, most, pieces=(), held_as=jnp.bfloat16):
    entries = jax.random.normal(stream_key, extent, jnp.float32) * width
    if len(pieces) > 0:
        entries = block_scale(stream_key, extent, pieces, -0.22, 0.18) * entries
    return jnp.clip(entries, min=-most, max=most).astype(held_as)


def setup_inputs(seed: int = 0, part: int = 0) -> dict:
    key_of = jax.random.split(jax.random.key(seed), 8)
    part_splits = jax.random.split(jax.random.fold_in(key_of[7], part), 8)
    object_tiles = centred(part_splits[0], (OH, 2, OW), 0.7, 4.0, ((0, 16),))
    probe = centred(key_of[1], (MODES, PATCH, 2, PATCH), 0.5, 3.0, (), jnp.float32)
    measured = jnp.clip(0.19921875 + 2.3007812 * jax.random.uniform(part_splits[2], (NPOS, PATCH, PATCH), jnp.float32) ** block_scale(part_splits[2], (NPOS, PATCH, PATCH), ((0, 16),), -0.2, 0.2), 0.19921875, 2.5).astype(jnp.bfloat16)
    offset_row = set_ends(jax.random.randint(part_splits[3], (NPOS,), 0, ROWS_DEV), jax.random.fold_in(part_splits[3], 1), 0, ROWS_DEV - 1).astype(jnp.int32)
    offset_col = set_ends(jax.random.randint(part_splits[4], (NPOS,), 0, OW - PATCH), jax.random.fold_in(part_splits[4], 1), 0, (OW - PATCH) - 1).astype(jnp.int32)
    subpixel = set_ends(jax.random.randint(part_splits[5], (NPOS,), 0, 16), jax.random.fold_in(part_splits[5], 1), 0, 15).astype(jnp.int32)
    live_count = uneven(part_splits[6], N_ROW, MINI, SLOTS, 2).astype(jnp.int32)
    return {"object_tiles": object_tiles, "probe": probe, "measured": measured, "offset_row": offset_row, "offset_col": offset_col, "subpixel": subpixel, "live_count": live_count}


def dft_tables(patch):
    index = jnp.arange(patch, dtype=jnp.int32)
    phase = index[:, None] * index[None, :] % patch
    angle = phase.astype(jnp.float32) * (2.0 * math.pi / patch)
    scale = 1.0 / math.sqrt(patch)
    cosine = (jnp.cos(angle) * scale).astype(jnp.bfloat16)
    sine = (jnp.sin(angle) * scale).astype(jnp.bfloat16)
    along_x = jnp.concatenate([jnp.concatenate([cosine, -sine], 1), jnp.concatenate([sine, cosine], 1)], 0)
    along_y = jnp.concatenate([jnp.stack([cosine, sine], -1).reshape(patch, 2 * patch), jnp.stack([-sine, cosine], -1).reshape(patch, 2 * patch)], 0)
    inverse_y = jnp.stack([jnp.concatenate([cosine, -sine], 1), jnp.concatenate([sine, cosine], 1)], 1).reshape(2 * patch, 2 * patch)
    inverse_x = jnp.concatenate([jnp.concatenate([cosine, sine], 1), jnp.concatenate([-sine, cosine], 1)], 0)
    return (along_x, along_y, inverse_y, inverse_x)

def fractions(code):
    return ((code // 4).astype(jnp.float32) * 0.25, (code % 4).astype(jnp.float32) * 0.25)

def interpolate(window, code):
    frac_y, frac_x = fractions(code)
    cells = window.astype(jnp.float32)
    size = cells.shape[0] - 1
    upper = (1.0 - frac_x) * cells[:size, :, :size] + frac_x * cells[:size, :, 1:]
    lower = (1.0 - frac_x) * cells[1:, :, :size] + frac_x * cells[1:, :, 1:]
    return (1.0 - frac_y) * upper + frac_y * lower

def spread(grad_patch, frac_y, frac_x):

    def sideways(part):
        return jnp.pad((1.0 - frac_x) * part, ((0, 0), (0, 0), (0, 1))) + jnp.pad(frac_x * part, ((0, 0), (0, 0), (1, 0)))
    upper = sideways((1.0 - frac_y) * grad_patch)
    lower = sideways(frac_y * grad_patch)
    return jnp.pad(upper, ((0, 1), (0, 0), (0, 0))) + jnp.pad(lower, ((1, 0), (0, 0), (0, 0)))

def slopes(window, grad_patch, frac_y, frac_x):
    cells = window.astype(jnp.float32)
    size = cells.shape[0] - 1
    down = cells[1:] - cells[:size]
    slope_y = (1.0 - frac_x) * down[:, :, :size] + frac_x * down[:, :, 1:]
    across = cells[:, :, 1:] - cells[:, :, :size]
    slope_x = (1.0 - frac_y) * across[:size] + frac_y * across[1:]
    return (jnp.sum(grad_patch * slope_y) / size, jnp.sum(grad_patch * slope_x) / size)

def matmul(left, right):
    return jnp.dot(left.astype(jnp.float32), right.astype(jnp.float32), precision=lax.Precision.HIGHEST)

def batched(left, right):
    return jnp.einsum('ab,mbk->mak', left.astype(jnp.float32), right.astype(jnp.float32), precision=lax.Precision.HIGHEST)

def project(patch_obj, amplitude, probe, tables):
    along_x, along_y, inverse_y, inverse_x = tables
    modes = probe.shape[0]
    size = probe.shape[1]
    preal = probe[:, :, 0, :]
    pimag = probe[:, :, 1, :]
    oreal = patch_obj[:, 0, :]
    oimag = patch_obj[:, 1, :]
    wave = jnp.stack([preal * oreal - pimag * oimag, preal * oimag + pimag * oreal], axis=2).astype(jnp.bfloat16)
    first = matmul(wave.reshape(modes * size, 2 * size), along_x).astype(jnp.bfloat16)
    far = batched(along_y, first.reshape(modes, 2 * size, size)).reshape(modes, 2, size, size)
    modulus = jnp.maximum(jnp.sqrt(lax.optimization_barrier(jnp.sum(far * far, axis=(0, 1)))), 0.5)
    ratio = 1.0 - amplitude.astype(jnp.float32) / modulus
    error = (far * ratio).astype(jnp.bfloat16)
    back = batched(inverse_y, error.reshape(modes, 2 * size, size)).astype(jnp.bfloat16)
    exit_grad = matmul(back.reshape(modes * size, 2 * size), inverse_x).reshape(modes, size, 2, size)
    ureal = exit_grad[:, :, 0, :]
    uimag = exit_grad[:, :, 1, :]
    obj_grad = jnp.stack([lax.optimization_barrier(jnp.sum(preal * ureal + pimag * uimag, 0)), lax.optimization_barrier(jnp.sum(preal * uimag - pimag * ureal, 0))], axis=1)
    probe_term = jnp.stack([oreal * ureal + oimag * uimag, oreal * uimag - oimag * ureal], axis=2)
    return (obj_grad, probe_term)

def reference(object_tiles, probe, measured, offset_row, offset_col, subpixel, live_count):
    size = PATCH
    padded = jnp.concatenate([object_tiles, jnp.zeros((size, 2, OW), object_tiles.dtype)], axis=0)
    tables = dft_tables(size)
    start = (jnp.zeros((OH + size, 2, OW), jnp.float32), jnp.zeros(probe.shape, jnp.float32), jnp.zeros((2, NPOS), jnp.float32))

    def device_pass(device, carry):
        device = jnp.asarray(device).astype(jnp.int32)

        def slot_pass(slot, inner):
            grad, probe_acc, moved = inner
            index = device * SLOTS + jnp.asarray(slot).astype(jnp.int32)
            top = (device * ROWS_DEV + offset_row[index]).astype(jnp.int32)
            left = offset_col[index].astype(jnp.int32)
            corner = (top, jnp.int32(0), left)
            window = lax.dynamic_slice(padded, corner, (size + 1, 2, size + 1))
            code = subpixel[index]
            frac_y, frac_x = fractions(code)
            obj_grad, probe_term = project(interpolate(window, code), measured[index], probe, tables)
            region = lax.dynamic_slice(grad, corner, (size + 1, 2, size + 1))
            grad = lax.dynamic_update_slice(grad, region + spread(obj_grad, frac_y, frac_x), corner)
            slope_y, slope_x = slopes(window, obj_grad, frac_y, frac_x)
            moved = moved.at[:, index].set(jnp.stack([slope_y, slope_x]))
            return (grad, probe_acc + probe_term, moved)
        return lax.fori_loop(0, live_count[device], slot_pass, carry)
    grad, probe_acc, moved = lax.fori_loop(0, N_ROW, device_pass, start)
    return (grad[:OH], probe_acc, moved)
```

```python
import functools
import math

import jax
import jax.numpy as jnp
import numpy as np
from jax import lax
from jax.experimental import pallas as pl
from jax.experimental.pallas import tpu as pltpu
from jax.sharding import PartitionSpec as P

LANES = 128
ROWS = 16


def passed_along(x, axis, by):
    length = lax.axis_size(axis)
    pairs = [(i, i + by) for i in range(length) if 0 <= i + by < length]
    return lax.ppermute(x, axis, pairs)


def summed(x, axis):
    length = lax.axis_size(axis)
    lines = x.size // x.shape[-1]
    if length & (length - 1) or lines % (length * ROWS):
        return lax.psum(x, axis)
    me = lax.axis_index(axis)
    part = x.reshape(length, lines // length, x.shape[-1])
    steps = [1 << k for k in range(length.bit_length() - 1)]

    def swap(y, step):
        return lax.ppermute(y, axis, [(i, i ^ step) for i in range(length)])

    for step in steps:
        many = part.shape[0] // 2
        bit = (me // step) % 2
        kept = lax.dynamic_slice_in_dim(part, bit * many, many, 0)
        sent = lax.dynamic_slice_in_dim(part, (1 - bit) * many, many, 0)
        part = kept + swap(sent.astype(jnp.bfloat16), step).astype(jnp.float32)
    part = part.astype(jnp.bfloat16)
    for step in reversed(steps):
        bit = (me // step) % 2
        other = swap(part, step)
        part = jnp.where(
            bit == 0, jnp.concatenate([part, other], 0), jnp.concatenate([other, part], 0)
        )
    return part.reshape(x.shape).astype(jnp.float32)


def dft_tables(patch):
    index = np.arange(patch)
    angle = ((index[:, None] * index[None, :]) % patch).astype(np.float64) * (2.0 * math.pi / patch)
    scale = 1.0 / math.sqrt(patch)
    cosine = jnp.asarray((np.cos(angle) * scale).astype(np.float32)).astype(jnp.bfloat16)
    sine = jnp.asarray((np.sin(angle) * scale).astype(np.float32)).astype(jnp.bfloat16)
    return cosine, sine


def pulled(x, by, tiles):
    lane = lax.broadcasted_iota(jnp.int32, x[0].shape, 1)
    back = lax.rem(LANES - by, LANES)
    parts = [pltpu.roll(x[k], back, 1) for k in range(tiles + 1)]
    keep = lane < LANES - by
    return [jnp.where(keep, parts[k], parts[k + 1]) for k in range(tiles)]


def pushed(x, by, tiles):
    lane = lax.broadcasted_iota(jnp.int32, (x.shape[0], LANES), 1)
    ahead = lax.rem(by, LANES)
    parts = [pltpu.roll(x[:, k * LANES : (k + 1) * LANES], ahead, 1) for k in range(tiles)]
    zero = jnp.zeros_like(parts[0])
    keep = lane >= by
    left = [zero] + parts
    right = parts + [zero]
    return [jnp.where(keep, right[k], left[k]) for k in range(tiles + 1)]


def step_kernel(
    modes, size, rows,
    count_ref, top_ref, left_ref, code_ref,
    own_hbm, rim_hbm, probe_ref, measured_ref, cos_ref, sin_ref,
    grad_ref, below_ref, pgrad_ref, moved_ref,
    ext, win, acc, table_a, table_b, patch, slope, far, power, gsum, sems,
):
    f32, bf16 = jnp.float32, jnp.bfloat16
    tiles = size // LANES
    slots = measured_ref.shape[0]
    wide = size + LANES
    copies = [
        pltpu.make_async_copy(own_hbm, ext.at[:, pl.ds(0, rows), :], sems.at[0]),
        pltpu.make_async_copy(rim_hbm, ext.at[:, pl.ds(rows, size), :], sems.at[1]),
    ]
    for copy in copies:
        copy.start()
    cosine, sine = cos_ref[...], sin_ref[...]
    table_a[0:size, 0:size] = cosine
    table_a[0:size, size : 2 * size] = -sine
    table_a[size : 2 * size, 0:size] = sine
    table_a[size : 2 * size, size : 2 * size] = cosine
    table_b[0:size, 0:size] = cosine
    table_b[0:size, size : 2 * size] = sine
    table_b[size : 2 * size, 0:size] = -sine
    table_b[size : 2 * size, size : 2 * size] = cosine
    pgrad_ref[...] = jnp.zeros_like(pgrad_ref)
    span = 32

    @pl.loop(0, (rows + size) // span)
    def _(i):
        at = pl.ds(pl.multiple_of(i * span, span), span)
        acc[:, :, at, :] = jnp.zeros((2, acc.shape[1], span, LANES), f32)

    for j in range(slots):
        moved_ref[0, j] = 0.0
        moved_ref[1, j] = 0.0
    for copy in copies:
        copy.wait()

    @pl.loop(0, count_ref[0])
    def _(j):
        top, left, code = top_ref[j], left_ref[j], code_ref[j]
        base_row = pl.multiple_of(top // ROWS * ROWS, ROWS)
        row = top - base_row
        base_col = pl.multiple_of(left // LANES * LANES, LANES)
        col = left - base_col
        fy = (code // 4).astype(f32) * 0.25
        fx = (code % 4).astype(f32) * 0.25
        cols = pl.ds(base_col, wide)
        chunk = 64

        for p in range(2):
            cut = ext[p, pl.ds(base_row, size + ROWS), cols].astype(f32)
            for k in range(tiles + 1):
                win[p, k] = cut[:, k * LANES : (k + 1) * LANES]

        @pl.loop(0, size // chunk)
        def _(i):
            at = pl.multiple_of(i * chunk, chunk)
            here = pl.ds(at, chunk)
            for p in range(2):
                v, d = [], []
                for k in range(tiles + 1):
                    upper = win[p, k, pl.ds(at + row, chunk), :]
                    lower = win[p, k, pl.ds(at + row + 1, chunk), :]
                    v.append((1.0 - fy) * upper + fy * lower)
                    d.append(lower - upper)
                v0, v1 = pulled(v, col, tiles), pulled(v, col + 1, tiles)
                d0, d1 = pulled(d, col, tiles), pulled(d, col + 1, tiles)
                for k in range(tiles):
                    to = pl.ds(k * LANES, LANES)
                    patch[p, here, to] = (1.0 - fx) * v0[k] + fx * v1[k]
                    slope[0, p, here, to] = (1.0 - fx) * d0[k] + fx * d1[k]
                    slope[1, p, here, to] = v1[k] - v0[k]

        power[...] = jnp.zeros_like(power)
        gsum[...] = jnp.zeros_like(gsum)

        @pl.loop(0, modes, unroll=True)
        def _(m):
            pr, pi = probe_ref[m, 0], probe_ref[m, 1]
            re, im = patch[0], patch[1]
            wave = jnp.concatenate(
                [(pr * re - pi * im).astype(bf16), (pr * im + pi * re).astype(bf16)], axis=1
            )
            half = jnp.dot(wave, table_a[...], preferred_element_type=f32).astype(bf16)
            stacked = jnp.concatenate([half[:, :size], half[:, size:]], axis=0)
            both = jnp.dot(table_b[...], stacked, preferred_element_type=f32)
            far[m] = both
            fr, fi = both[:size], both[size:]
            power[...] += fr * fr + fi * fi

        modulus = jnp.maximum(jnp.sqrt(power[...]), 0.5)
        power[...] = 1.0 - measured_ref[j].astype(f32) / modulus

        @pl.loop(0, modes, unroll=True)
        def _(m):
            ratio = power[...]
            error = jnp.concatenate(
                [(far[m, :size] * ratio).astype(bf16), (far[m, size:] * ratio).astype(bf16)], axis=0
            )
            back = jnp.dot(table_a[...], error, preferred_element_type=f32).astype(bf16)
            side = jnp.concatenate([back[:size], back[size:]], axis=1)
            exit_grad = jnp.dot(side, table_b[...], preferred_element_type=f32)
            ur, ui = exit_grad[:, :size], exit_grad[:, size:]
            pr, pi = probe_ref[m, 0], probe_ref[m, 1]
            re, im = patch[0], patch[1]
            gsum[0] += pr * ur + pi * ui
            gsum[1] += pr * ui - pi * ur
            pgrad_ref[m, 0] += re * ur + im * ui
            pgrad_ref[m, 1] += re * ui - im * ur

        for s in range(2):
            total = jnp.sum(gsum[0] * slope[s, 0] + gsum[1] * slope[s, 1])
            moved_ref[s, j] = total / size

        @pl.loop(0, size // chunk)
        def _(i):
            at = pl.multiple_of(i * chunk, chunk)
            for p in range(2):
                g = gsum[p, pl.ds(at, chunk), :]
                s0, s1 = pushed(g, col, tiles), pushed(g, col + 1, tiles)
                for k in range(tiles + 1):
                    s = (1.0 - fx) * s0[k] + fx * s1[k]
                    tile = left // LANES + k
                    acc[p, tile, pl.ds(top + at, chunk), :] += (1.0 - fy) * s
                    acc[p, tile, pl.ds(top + at + 1, chunk), :] += fy * s

    @pl.loop(0, rows // span)
    def _(i):
        at = pl.multiple_of(i * span, span)
        for k in range(acc.shape[1]):
            grad_ref[:, pl.ds(at, span), pl.ds(k * LANES, LANES)] = acc[:, k, pl.ds(at, span), :]

    @pl.loop(0, size // span)
    def _(i):
        at = pl.multiple_of(i * span, span)
        for k in range(acc.shape[1]):
            below_ref[:, pl.ds(at, span), pl.ds(k * LANES, LANES)] = acc[
                :, k, pl.ds(rows + at, span), :
            ].astype(bf16)


def shards(object_tiles, probe, measured, offset_row, offset_col, subpixel, live_count):
    f32, bf16 = jnp.float32, jnp.bfloat16
    rows, _, width = object_tiles.shape
    modes, size = probe.shape[:2]
    slots = measured.shape[0]
    own = jnp.transpose(object_tiles, (1, 0, 2))
    rim = passed_along(own[:, :size], "row", -1)
    probe_planes = jnp.transpose(probe, (0, 2, 1, 3))
    cosine, sine = dft_tables(size)
    vmem = pl.BlockSpec(memory_space=pltpu.VMEM)
    smem = pl.BlockSpec(memory_space=pltpu.SMEM)
    hbm = pl.BlockSpec(memory_space=pl.ANY)
    grad, below, probe_sum, moved = pl.pallas_call(
        functools.partial(step_kernel, modes, size, rows),
        out_shape=(
            jax.ShapeDtypeStruct((2, rows, width), f32),
            jax.ShapeDtypeStruct((2, size, width), bf16),
            jax.ShapeDtypeStruct((modes, 2, size, size), f32),
            jax.ShapeDtypeStruct((2, slots), f32),
        ),
        in_specs=[smem] * 4 + [hbm] * 2 + [vmem] * 4,
        out_specs=(vmem, vmem, vmem, smem),
        scratch_shapes=[
            pltpu.VMEM((2, rows + size, width), bf16),
            pltpu.VMEM((2, size // LANES + 1, size + ROWS, LANES), f32),
            pltpu.VMEM((2, width // LANES, rows + size, LANES), f32),
            pltpu.VMEM((2 * size, 2 * size), bf16),
            pltpu.VMEM((2 * size, 2 * size), bf16),
            pltpu.VMEM((2, size, size), f32),
            pltpu.VMEM((2, 2, size, size), f32),
            pltpu.VMEM((modes, 2 * size, size), f32),
            pltpu.VMEM((size, size), f32),
            pltpu.VMEM((2, size, size), f32),
            pltpu.SemaphoreType.DMA((2,)),
        ],
        compiler_params=pltpu.CompilerParams(vmem_limit_bytes=60 << 20),
        name="step",
    )(live_count, offset_row, offset_col, subpixel, own, rim, probe_planes, measured, cosine, sine)
    landed = passed_along(below, "row", 1)
    probe_grad = jnp.transpose(summed(probe_sum, "row"), (0, 2, 1, 3))
    grad = grad.at[:, :size].add(landed.astype(f32))
    return (jnp.transpose(grad, (1, 0, 2)), probe_grad, moved)


def solution(mesh):
    in_specs = (
        P(("groups", "row"), None, None),
        P(),
        P(("groups", "row"), None, None),
        P(("groups", "row")),
        P(("groups", "row")),
        P(("groups", "row")),
        P(("groups", "row")),
    )
    out_specs = (
        P(("groups", "row"), None, None),
        P("groups", None, None, None),
        P(None, ("groups", "row")),
    )
    return jax.shard_map(shards, mesh=mesh, in_specs=in_specs, out_specs=out_specs, check_vma=False)
```
